256 devices in a mesh: section: 4 (over y), dp: 16 (over x, z_lo, core), expert: 4 (over z_hi).
Axes of the slice: x: 4, y: 4, z: 8 (z_hi: 4, z_lo: 2; z = z_hi * 2 + z_lo), core: 2. Of those that a mesh axis runs over, the one named last changes fastest.
Arguments:
- init_state: bfloat16 [4, 2048, 5280], P(None, ('dp', 'expert')), may hold values from -5 to 5
- inject: bfloat16 [4, 2048, 5280], P(None, ('dp', 'expert')), may hold values from -24 to 24
- routes: int32 [2, 4, 4, 2048, 1], P(None, 'section', None, ('dp', 'expert')), may hold values from 0 to 3; in each aligned block of 32 rows (0 to 31, 32 to 63, ..., all dimensions but the last counted through in order) at most 12 rows name the same one
- norm_gain: float32 [4, 5280], P('section'), may hold values from 0.25 to 1.75
- router: bfloat16 [4, 4, 5280], P('section'), may hold values from -0.078125 to 0.078125
- w_up: bfloat16 [4, 4, 5280, 768], P('section', 'expert', 'dp'), may hold values from -0.078125 to 0.078125
- w_down: bfloat16 [4, 4, 768, 5280], P('section', 'expert', None, 'dp'), may hold values from -0.21875 to 0.21875
Outputs:
- final_state: bfloat16 [4, 2048, 5280], P('section', ('dp', 'expert'))
The draws below stay inside these ranges and needn't reach their ends.
Inputs may be any that keep to these rules, and one draw needn't show every extreme that they name: In each aligned block of 32 tokens of routes, no expert is named by more than 12 tokens.
All inputs are finite; a program needn't handle non-finite values.
Results may differ from the reference program's by a relative error of at most 0.014.
Values may be sent and summed in bfloat16 or wider, within the bound.
A program may use at most 128 MiB of HBM per device.

```python
import math
import jax
import jax.numpy as jnp
import numpy as np
from jax import lax

D = 5280
F = 768
TOK_DEV = 32
RECUR = 2
CAP = 12
EXPERTS = 4
MICRO = 4
MBT = 2048
N_SECTION = 4
N_DP = 16
N_EXPERT = 4


def draw_inject(key, part):
    streams = jax.random.split(key, 3)
    extent = (MICRO, MBT, D)
    values = jnp.clip(jax.random.normal(streams[0], extent, jnp.float32), -4.0, 4.0)
    lowest = math.log(0.5)
    highest = math.log(2.0)
    row_scale = jnp.exp(jax.random.uniform(streams[1], (MICRO, MBT, 1), jnp.float32, lowest, highest))
    col_scale = jnp.exp(jax.random.uniform(streams[2], (1, 1, D), jnp.float32, lowest, highest))
    return (values * row_scale * col_scale).astype(jnp.bfloat16)


def shard_levels(stream_key, dims, shards, low, top_value):
    def one(axis_at, shards_of):
        steps = jax.random.uniform(jax.random.fold_in(jax.random.fold_in(stream_key, 6), axis_at), (shards_of,), jnp.float32, low / len(shards), top_value / len(shards))
        return jnp.repeat(jnp.exp(steps), dims[axis_at] // shards_of).reshape((-1,) + (1,) * (len(dims) - axis_at - 1))

    loudness = one(*shards[0])
    for cut in shards[1:]:
        loudness = loudness * one(*cut)
    return loudness


def shared_out(key, own, number, rows, count, top, reach, skew):
    sequence = jax.random.permutation(key, count)
    heavy_load, common = shares(count, rows * top, reach, skew, True), shares(count, rows * top, reach, skew, False)
    places = jnp.arange(count)

    def named(sizes, rotation):
        used = int((sizes > 0).sum())
        fixed = max(1, used // 4)
        moved = fixed + (places - fixed + rotation * (used - fixed)) % max(1, count - fixed)
        return jnp.zeros((count,), jnp.int32).at[sequence[jnp.where(places < fixed, places, moved)]].set(jnp.asarray(sizes, jnp.int32))

    sizes = jnp.where(number % 4 == 0, named(heavy_load, number // 4), named(common, number - number // 4 - 1))
    mixed = jax.random.permutation(jax.random.fold_in(own, 3), count)
    source_of, receiver = mixed[0:count // 2 * 2:2], mixed[1:count // 2 * 2:2]
    slack = jnp.minimum(sizes[source_of] - 1, reach - sizes[receiver]) // 2
    slack = jnp.where((source_of == sequence[0]) | (receiver == sequence[0]) | (sizes[receiver] == 0), 0, jnp.maximum(slack, 0))
    moved = jax.random.randint(jax.random.fold_in(own, 4), (count // 2,), 0, 1 << 20) % (slack + 1)
    sizes = sizes.at[source_of].add(-moved).at[receiver].add(moved)
    members = jnp.searchsorted(jnp.cumsum(sizes), jnp.arange(rows * top), side="right").astype(jnp.int32)
    listing = members.reshape(top, rows).T
    listing = listing[jax.random.permutation(jax.random.fold_in(own, 1), rows)]
    rotation = jax.random.randint(jax.random.fold_in(own, 2), (rows, 1), 0, top)
    return jnp.take_along_axis(listing, (jnp.arange(top)[None, :] + rotation) % top, axis=1)


def shares(number_of, total, limit, lean, full):
    portions = [(1 << 20) // math.isqrt(rank ** lean) + 1 for rank in range(1, number_of + 1)]
    largest = limit if full else min(limit, max(-(-total // number_of), total * portions[0] // sum(portions)))
    least = 1 if total - largest >= number_of - 1 else 0
    counts, spare = [largest] + [least] * (number_of - 1), total - largest - least * (number_of - 1)
    while spare > 0:
        free = [i for i in range(1, number_of) if counts[i] < largest] or [i for i in range(1, number_of) if counts[i] < limit]
        mass, budget = sum([portions[i] for i in free]), spare
        for i in free:
            addition = min(limit - counts[i], max(1, budget * portions[i] // mass), spare)
            counts[i] = counts[i] + addition
            spare = spare - addition
    return np.array(counts)


def bell_draw(own_key, shape, deviation, bound, cuts=(), held_as=jnp.bfloat16):
    drawn = deviation * jax.random.normal(own_key, shape, jnp.float32)
    if cuts:
        drawn = drawn * shard_levels(own_key, shape, cuts, -0.22, 0.18)
    return jnp.clip(drawn, -bound, bound).astype(held_as)


def setup_inputs(seed: int = 0) -> dict:
    key_list = jax.random.split(jax.random.key(seed), 8)
    init_state = bell_draw(key_list[0], (MICRO, MBT, D), 1.0, 5.0, ((1, 64),))
    inject = draw_inject(jax.random.fold_in(key_list[7], 71), 0)
    routes_keys = jax.random.split(jax.random.fold_in(key_list[2], 1), RECUR * N_SECTION * MICRO * MBT // TOK_DEV)
    routes_turns = jax.random.permutation(jax.random.fold_in(key_list[2], 3), RECUR * N_SECTION * MICRO * MBT // TOK_DEV)
    routes = jax.vmap(lambda own, number: shared_out(jax.random.fold_in(key_list[2], 2), own, number, TOK_DEV, EXPERTS, 1, CAP, 1))(routes_keys, routes_turns).reshape((RECUR, N_SECTION, MICRO, MBT, 1))
    norm_gain = jnp.clip(1.0 + 0.15 * jax.random.normal(key_list[3], (N_SECTION, D), jnp.float32), 0.25, 1.75)
    router = bell_draw(key_list[4], (N_SECTION, EXPERTS, D), D ** -0.5, 0.078125, ((0, 4),))
    w_up = bell_draw(key_list[5], (N_SECTION, EXPERTS, D, F), D ** -0.5, 0.078125, ((0, 4), (1, 4), (2, 16)))
    w_down = bell_draw(key_list[6], (N_SECTION, EXPERTS, F, D), F ** -0.5, 0.21875, ((0, 4), (1, 4), (3, 16)))
    return {"init_state": init_state, "inject": inject, "routes": routes, "norm_gain": norm_gain, "router": router, "w_up": w_up, "w_down": w_down}


def core_block(current, gain_row, router_rows, up_stack, down_stack, assign):
    as_float = current.astype(jnp.float32)
    inv_rms = lax.rsqrt(lax.optimization_barrier(jnp.mean(as_float * as_float, axis=-1, keepdims=True)) + 1e-05)
    normed = (as_float * inv_rms * gain_row).astype(jnp.bfloat16)
    logits = jnp.dot(normed, router_rows.T, preferred_element_type=jnp.float32)
    labels = jnp.arange(EXPERTS, dtype=jnp.int32)
    member = assign[:, None] == labels[None, :]
    gate_value = jax.nn.sigmoid(lax.optimization_barrier(jnp.sum(jnp.where(member, logits, jnp.float32(0.0)), axis=-1)))
    row_limit = N_DP * N_EXPERT * CAP
    collected = jnp.zeros(as_float.shape, jnp.float32)
    for expert_id in range(EXPERTS):
        chosen_mask = assign == expert_id
        chosen = jnp.nonzero(chosen_mask, size=row_limit, fill_value=0)[0].astype(jnp.int32)
        is_valid = jnp.arange(row_limit, dtype=jnp.int32) < jnp.sum(chosen_mask.astype(jnp.int32))
        picked_rows = normed[chosen]
        hidden = jax.nn.gelu(jnp.dot(picked_rows, up_stack[expert_id], preferred_element_type=jnp.float32)).astype(jnp.bfloat16)
        expert_out = jnp.dot(hidden, down_stack[expert_id], preferred_element_type=jnp.float32).astype(jnp.bfloat16)
        collected = collected.at[chosen].add(jnp.where(is_valid[:, None], expert_out.astype(jnp.float32), jnp.float32(0.0)))
    return (as_float + gate_value[:, None] * collected).astype(jnp.bfloat16)

def reference(init_state, inject, routes, norm_gain, router, w_up, w_down):
    finals = []
    for micro_idx in range(MICRO):
        current = (init_state[micro_idx].astype(jnp.float32) + inject[micro_idx].astype(jnp.float32)).astype(jnp.bfloat16)
        for round_idx in range(RECUR):
            if round_idx > 0:
                current = (current.astype(jnp.float32) + inject[micro_idx].astype(jnp.float32)).astype(jnp.bfloat16)
            for block_idx in range(N_SECTION):
                current = core_block(current, norm_gain[block_idx], router[block_idx], w_up[block_idx], w_down[block_idx], routes[round_idx, block_idx, micro_idx, :, 0])
        finals.append(current)
    return jnp.stack(finals)
```

```python
import jax
import jax.numpy as jnp
from jax import lax
from jax.sharding import PartitionSpec as P

RECUR = 2
CAP = 12


def shifted(block, axis, distance):
    devices = range(lax.axis_size(axis))
    route = [((i - distance) % len(devices), i) for i in devices]
    return lax.ppermute(block, axis, route)


def normalize(current, gain_row):
    as_float = current.astype(jnp.float32)
    inv_rms = lax.rsqrt(jnp.mean(as_float * as_float, axis=-1, keepdims=True) + 1e-05)
    return (as_float * inv_rms * gain_row).astype(jnp.bfloat16)


def expert_rows(item_rows, w_first, w_second):
    extent = item_rows.shape
    flat_rows = item_rows.reshape(-1, extent[-1])
    hidden = jax.nn.gelu(jnp.dot(flat_rows, w_first, preferred_element_type=jnp.float32)).astype(
        jnp.bfloat16
    )
    result = jnp.dot(hidden, w_second, preferred_element_type=jnp.float32).astype(jnp.bfloat16)
    return result.reshape(extent)


def whole_round(buffer, w_first, w_second):
    groups = buffer.shape[0]
    arrived = jnp.stack([buffer[0]] + [shifted(buffer[j], "expert", j) for j in range(1, groups)])
    processed = expert_rows(arrived, w_first, w_second)
    return jnp.stack(
        [processed[0]] + [shifted(processed[j], "expert", groups - j) for j in range(1, groups)]
    )


def core_block(current, gain_row, router_rows, w_first, w_second, assign):
    tokens = current.shape[0]
    experts = router_rows.shape[0]
    normed = normalize(current, gain_row)
    logits = jnp.dot(normed, router_rows.T, preferred_element_type=jnp.float32)
    labels = lax.broadcasted_iota(jnp.int32, (tokens, experts), 1)
    onehot = (assign[:, None] == labels).astype(jnp.float32)
    gate_value = jax.nn.sigmoid(jnp.sum(onehot * logits, axis=-1))
    earlier = (
        lax.broadcasted_iota(jnp.int32, (tokens, tokens), 0)
        > lax.broadcasted_iota(jnp.int32, (tokens, tokens), 1)
    ).astype(jnp.float32)
    counts = jnp.dot(earlier, onehot, preferred_element_type=jnp.float32)
    slot_index = jnp.sum(onehot * counts, axis=-1).astype(jnp.int32)
    relative = jnp.mod(assign - lax.axis_index("expert"), experts)
    target = relative * CAP + slot_index
    places = (
        lax.broadcasted_iota(jnp.int32, (experts * CAP, tokens), 0) == target[None, :]
    ).astype(jnp.bfloat16)
    buffer = (
        jnp.dot(places, normed, preferred_element_type=jnp.float32)
        .astype(jnp.bfloat16)
        .reshape(experts, CAP, -1)
    )
    returned = whole_round(buffer, w_first, w_second)
    flat_back = returned.reshape(experts * CAP, -1)
    expert_out = jnp.einsum("st,sd->td", places, flat_back, preferred_element_type=jnp.float32)
    updated = current.astype(jnp.float32) + gate_value[:, None] * expert_out
    return updated.astype(jnp.bfloat16)


def body(init_state, inject, routes, norm_gain, router, w_up, w_down):
    sections = lax.axis_size("section")
    section_index = lax.axis_index("section")
    up_all, down_all = (
        lax.all_gather(w_up, "dp", axis=2, tiled=True),
        lax.all_gather(w_down, "dp", axis=3, tiled=True),
    )
    w_first = up_all[0, 0]
    w_second = down_all[0, 0]
    gain_row = norm_gain[0]
    router_rows = router[0]
    tokens = init_state.shape[1]
    active_span = sections * RECUR
    total_steps = active_span + sections - 1

    def advance(moment, hidden_state):
        offset = moment - section_index
        is_live = (offset >= 0) & (offset < active_span)
        clipped = jnp.clip(offset, 0, active_span - 1)
        loop_round = clipped // sections
        entry_slot = clipped % sections
        micro_idx = jnp.mod(sections - 2 - entry_slot, sections)
        initial = lax.dynamic_index_in_dim(init_state, micro_idx, 0, keepdims=False)
        injected_row = lax.dynamic_index_in_dim(inject, micro_idx, 0, keepdims=False)
        incoming = jnp.where(loop_round == 0, initial, hidden_state)
        injected = (incoming.astype(jnp.float32) + injected_row.astype(jnp.float32)).astype(
            jnp.bfloat16
        )
        entering = is_live & (section_index == 0)
        current = jnp.where(entering, injected, hidden_state)
        assign = lax.dynamic_slice(
            routes, (loop_round, 0, micro_idx, 0, 0), (1, 1, 1, tokens, 1)
        ).reshape(tokens)
        result = core_block(current, gain_row, router_rows, w_first, w_second, assign)
        return jnp.where(is_live, result, hidden_state)

    def advance_one(moment, hidden_state):
        arrived = shifted(hidden_state, "section", 1)
        return advance(moment, arrived)

    hidden_state = jnp.zeros(init_state.shape[1:], jnp.bfloat16)
    hidden_state = advance(0, hidden_state)
    hidden_state = lax.fori_loop(1, total_steps, advance_one, hidden_state)
    return hidden_state[None]


def solution(mesh):
    return jax.shard_map(
        body,
        mesh=mesh,
        in_specs=(
            P(None, ("dp", "expert"), None),
            P(None, ("dp", "expert"), None),
            P(None, "section", None, ("dp", "expert"), None),
            P("section", None),
            P("section", None, None),
            P("section", "expert", "dp", None),
            P("section", "expert", None, "dp"),
        ),
        out_specs=P("section", ("dp", "expert"), None),
        check_vma=False,
    )
```

```python
import functools

import jax
import jax.numpy as jnp
from jax import lax
from jax.experimental import pallas as pl
from jax.experimental.pallas import tpu as pltpu
from jax.sharding import PartitionSpec as P

MESH = pl.DeviceIdType.MESH

RECUR = 2
CAP = 12


def shifted(block, axis, distance):
    devices = range(lax.axis_size(axis))
    route = [((i - distance) % len(devices), i) for i in devices]
    return lax.ppermute(block, axis, route)


def normalize(current, gain_row):
    as_float = current.astype(jnp.float32)
    inv_rms = lax.rsqrt(jnp.mean(as_float * as_float, axis=-1, keepdims=True) + 1e-05)
    return (as_float * inv_rms * gain_row).astype(jnp.bfloat16)


def expert_rows(item_rows, w_first, w_second):
    extent = item_rows.shape
    flat_rows = item_rows.reshape(-1, extent[-1])
    hidden = jax.nn.gelu(jnp.dot(flat_rows, w_first, preferred_element_type=jnp.float32)).astype(
        jnp.bfloat16
    )
    result = jnp.dot(hidden, w_second, preferred_element_type=jnp.float32).astype(jnp.bfloat16)
    return result.reshape(extent)


def exchange_kernel(direction, src_ref, dst_ref, send_sem, recv_sem):
    groups = src_ref.shape[0]
    me = lax.axis_index("expert")
    place = (lax.axis_index("section"), lax.axis_index("dp"))
    barrier = pltpu.get_barrier_semaphore()
    for j in range(1, groups):
        pl.semaphore_signal(
            barrier, inc=1, device_id=place + (lax.rem(me + j, groups),), device_id_type=MESH
        )
    pl.semaphore_wait(barrier, groups - 1)
    copies = []
    for j in range(1, groups):
        target = lax.rem(me + direction * j + groups, groups)
        copy = pltpu.make_async_remote_copy(
            src_ref=src_ref.at[j],
            dst_ref=dst_ref.at[j],
            send_sem=send_sem.at[j - 1],
            recv_sem=recv_sem.at[j - 1],
            device_id=place + (target,),
            device_id_type=MESH,
        )
        copy.start()
        copies.append(copy)
    dst_ref[0] = src_ref[0]
    for copy in copies:
        copy.wait()


def exchange(buffer, direction, channel):
    groups = buffer.shape[0]
    return pl.pallas_call(
        functools.partial(exchange_kernel, direction),
        out_shape=jax.ShapeDtypeStruct(buffer.shape, buffer.dtype),
        in_specs=[pl.BlockSpec(memory_space=pltpu.VMEM)],
        out_specs=pl.BlockSpec(memory_space=pltpu.VMEM),
        scratch_shapes=[
            pltpu.SemaphoreType.DMA((groups - 1,)),
            pltpu.SemaphoreType.DMA((groups - 1,)),
        ],
        compiler_params=pltpu.CompilerParams(collective_id=channel, has_side_effects=True),
    )(buffer)


def whole_round(buffer, w_first, w_second):
    arrived = exchange(buffer, 1, 0)
    processed = expert_rows(arrived, w_first, w_second)
    return exchange(processed, -1, 1)


def core_block(current, gain_row, router_rows, w_first, w_second, assign):
    tokens = current.shape[0]
    experts = router_rows.shape[0]
    normed = normalize(current, gain_row)
    logits = jnp.dot(normed, router_rows.T, preferred_element_type=jnp.float32)
    labels = lax.broadcasted_iota(jnp.int32, (tokens, experts), 1)
    onehot = (assign[:, None] == labels).astype(jnp.float32)
    gate_value = jax.nn.sigmoid(jnp.sum(onehot * logits, axis=-1))
    earlier = (
        lax.broadcasted_iota(jnp.int32, (tokens, tokens), 0)
        > lax.broadcasted_iota(jnp.int32, (tokens, tokens), 1)
    ).astype(jnp.float32)
    counts = jnp.dot(earlier, onehot, preferred_element_type=jnp.float32)
    slot_index = jnp.sum(onehot * counts, axis=-1).astype(jnp.int32)
    relative = jnp.mod(assign - lax.axis_index("expert"), experts)
    target = relative * CAP + slot_index
    places = (
        lax.broadcasted_iota(jnp.int32, (experts * CAP, tokens), 0) == target[None, :]
    ).astype(jnp.bfloat16)
    buffer = (
        jnp.dot(places, normed, preferred_element_type=jnp.float32)
        .astype(jnp.bfloat16)
        .reshape(experts, CAP, -1)
    )
    returned = whole_round(buffer, w_first, w_second)
    flat_back = returned.reshape(experts * CAP, -1)
    expert_out = jnp.einsum("st,sd->td", places, flat_back, preferred_element_type=jnp.float32)
    updated = current.astype(jnp.float32) + gate_value[:, None] * expert_out
    return updated.astype(jnp.bfloat16)


def body(init_state, inject, routes, norm_gain, router, w_up, w_down):
    sections = lax.axis_size("section")
    section_index = lax.axis_index("section")
    up_all, down_all = (
        lax.all_gather(w_up, "dp", axis=2, tiled=True),
        lax.all_gather(w_down, "dp", axis=3, tiled=True),
    )
    w_first = up_all[0, 0]
    w_second = down_all[0, 0]
    gain_row = norm_gain[0]
    router_rows = router[0]
    tokens = init_state.shape[1]
    active_span = sections * RECUR
    total_steps = active_span + sections - 1

    def advance(moment, hidden_state):
        offset = moment - section_index
        is_live = (offset >= 0) & (offset < active_span)
        clipped = jnp.clip(offset, 0, active_span - 1)
        loop_round = clipped // sections
        entry_slot = clipped % sections
        micro_idx = jnp.mod(sections - 2 - entry_slot, sections)
        initial = lax.dynamic_index_in_dim(init_state, micro_idx, 0, keepdims=False)
        injected_row = lax.dynamic_index_in_dim(inject, micro_idx, 0, keepdims=False)
        incoming = jnp.where(loop_round == 0, initial, hidden_state)
        injected = (incoming.astype(jnp.float32) + injected_row.astype(jnp.float32)).astype(
            jnp.bfloat16
        )
        entering = is_live & (section_index == 0)
        current = jnp.where(entering, injected, hidden_state)
        assign = lax.dynamic_slice(
            routes, (loop_round, 0, micro_idx, 0, 0), (1, 1, 1, tokens, 1)
        ).reshape(tokens)
        result = core_block(current, gain_row, router_rows, w_first, w_second, assign)
        return jnp.where(is_live, result, hidden_state)

    def advance_one(moment, hidden_state):
        arrived = shifted(hidden_state, "section", 1)
        return advance(moment, arrived)

    hidden_state = jnp.zeros(init_state.shape[1:], jnp.bfloat16)
    hidden_state = advance(0, hidden_state)
    hidden_state = lax.fori_loop(1, total_steps, advance_one, hidden_state)
    return hidden_state[None]


def solution(mesh):
    return jax.shard_map(
        body,
        mesh=mesh,
        in_specs=(
            P(None, ("dp", "expert"), None),
            P(None, ("dp", "expert"), None),
            P(None, "section", None, ("dp", "expert"), None),
            P("section", None),
            P("section", None, None),
            P("section", "expert", "dp", None),
            P("section", "expert", None, "dp"),
        ),
        out_specs=P("section", ("dp", "expert"), None),
        check_vma=False,
    )
```

```python
import functools

import jax
import jax.numpy as jnp
from jax import lax
from jax.experimental import pallas as pl
from jax.experimental.pallas import tpu as pltpu
from jax.sharding import PartitionSpec as P

MESH = pl.DeviceIdType.MESH

RECUR = 2
CAP = 12


def shifted(block, axis, distance):
    devices = range(lax.axis_size(axis))
    route = [((i - distance) % len(devices), i) for i in devices]
    return lax.ppermute(block, axis, route)


def normalize(current, gain_row):
    as_float = current.astype(jnp.float32)
    inv_rms = lax.rsqrt(jnp.mean(as_float * as_float, axis=-1, keepdims=True) + 1e-05)
    return (as_float * inv_rms * gain_row).astype(jnp.bfloat16)


def expert_rows(item_rows, w_first, w_second):
    extent = item_rows.shape
    flat_rows = item_rows.reshape(-1, extent[-1])
    hidden = jax.nn.gelu(jnp.dot(flat_rows, w_first, preferred_element_type=jnp.float32)).astype(
        jnp.bfloat16
    )
    result = lax.dot_general(
        hidden, w_second, (((1,), (1,)), ((), ())), preferred_element_type=jnp.float32
    ).astype(jnp.bfloat16)
    return result.reshape(extent)


def neighbour(delta):
    experts = lax.axis_size("expert")
    dp = lax.axis_index("dp")
    half = lax.rem(dp // 2, 2)
    chip = lax.axis_index("expert") * 2 + half
    target = lax.rem(chip + delta + 2 * experts, 2 * experts)
    shifted_dp = dp + (lax.rem(target, 2) - half) * 2
    return (lax.axis_index("section"), shifted_dp, target // 2)


def dispatch_delta(group):
    half = lax.rem(lax.axis_index("dp") // 2, 2)
    return group * (1 if group == 2 else -1) * (1 - 2 * half)


def return_delta(group):
    half = lax.rem(lax.axis_index("dp") // 2, 2)
    return group * (2 * half - 1)


def exchange_kernel(outgoing, incoming, src_ref, dst_ref, send_sem, recv_sem):
    groups = src_ref.shape[0]
    barrier = pltpu.get_barrier_semaphore()
    for j in range(1, groups):
        pl.semaphore_signal(
            barrier, inc=1, device_id=neighbour(incoming(j)), device_id_type=MESH
        )
    pl.semaphore_wait(barrier, groups - 1)
    copies = []
    for j in range(1, groups):
        copy = pltpu.make_async_remote_copy(
            src_ref=src_ref.at[j],
            dst_ref=dst_ref.at[j],
            send_sem=send_sem.at[j - 1],
            recv_sem=recv_sem.at[j - 1],
            device_id=neighbour(outgoing(j)),
            device_id_type=MESH,
        )
        copy.start()
        copies.append(copy)
    dst_ref[0] = src_ref[0]
    for copy in copies:
        copy.wait()


def exchange(buffer, outgoing, incoming, channel):
    groups = buffer.shape[0]
    return pl.pallas_call(
        functools.partial(exchange_kernel, outgoing, incoming),
        out_shape=jax.ShapeDtypeStruct(buffer.shape, buffer.dtype),
        in_specs=[pl.BlockSpec(memory_space=pltpu.VMEM)],
        out_specs=pl.BlockSpec(memory_space=pltpu.VMEM),
        scratch_shapes=[
            pltpu.SemaphoreType.DMA((groups - 1,)),
            pltpu.SemaphoreType.DMA((groups - 1,)),
        ],
        compiler_params=pltpu.CompilerParams(collective_id=channel, has_side_effects=True),
    )(buffer)


def group_of(assign, experts):
    relative = jnp.mod(assign - lax.axis_index("expert"), experts)
    half = lax.rem(lax.axis_index("dp") // 2, 2)
    swapped = jnp.where((relative == 1) == (half == 0), 2, 1)
    return jnp.where(relative == 2, 3, jnp.where(relative == 0, 0, swapped))


def whole_round(buffer, w_first, w_second):
    arrived = exchange(buffer, dispatch_delta, return_delta, 0)
    processed = expert_rows(arrived, w_first, w_second)
    return exchange(processed, return_delta, dispatch_delta, 1)


def core_block(current, gain_row, router_rows, w_first, w_second, assign):
    tokens = current.shape[0]
    experts = router_rows.shape[0]
    normed = normalize(current, gain_row)
    logits = jnp.dot(normed, router_rows.T, preferred_element_type=jnp.float32)
    labels = lax.broadcasted_iota(jnp.int32, (tokens, experts), 1)
    onehot = (assign[:, None] == labels).astype(jnp.float32)
    gate_value = jax.nn.sigmoid(jnp.sum(onehot * logits, axis=-1))
    earlier = (
        lax.broadcasted_iota(jnp.int32, (tokens, tokens), 0)
        > lax.broadcasted_iota(jnp.int32, (tokens, tokens), 1)
    ).astype(jnp.float32)
    counts = jnp.dot(earlier, onehot, preferred_element_type=jnp.float32)
    slot_index = jnp.sum(onehot * counts, axis=-1).astype(jnp.int32)
    target = group_of(assign, experts) * CAP + slot_index
    places = (
        lax.broadcasted_iota(jnp.int32, (experts * CAP, tokens), 0) == target[None, :]
    ).astype(jnp.bfloat16)
    buffer = (
        jnp.dot(places, normed, preferred_element_type=jnp.float32)
        .astype(jnp.bfloat16)
        .reshape(experts, CAP, -1)
    )
    returned = whole_round(buffer, w_first, w_second)
    flat_back = returned.reshape(experts * CAP, -1)
    expert_out = jnp.einsum("st,sd->td", places, flat_back, preferred_element_type=jnp.float32)
    updated = current.astype(jnp.float32) + gate_value[:, None] * expert_out
    return updated.astype(jnp.bfloat16)


def body(init_state, inject, routes, norm_gain, router, w_up, w_down):
    sections = lax.axis_size("section")
    section_index = lax.axis_index("section")
    up_all, down_all = (
        lax.all_gather(w_up, "dp", axis=2, tiled=True),
        lax.all_gather(jnp.swapaxes(w_down, 2, 3), "dp", axis=2, tiled=True),
    )
    w_first = up_all[0, 0]
    w_second = down_all[0, 0]
    gain_row = norm_gain[0]
    router_rows = router[0]
    tokens = init_state.shape[1]
    active_span = sections * RECUR
    total_steps = active_span + sections - 1

    def advance(moment, hidden_state):
        offset = moment - section_index
        is_live = (offset >= 0) & (offset < active_span)
        clipped = jnp.clip(offset, 0, active_span - 1)
        loop_round = clipped // sections
        entry_slot = clipped % sections
        micro_idx = jnp.mod(sections - 2 - entry_slot, sections)
        initial = lax.dynamic_index_in_dim(init_state, micro_idx, 0, keepdims=False)
        injected_row = lax.dynamic_index_in_dim(inject, micro_idx, 0, keepdims=False)
        incoming = jnp.where(loop_round == 0, initial, hidden_state)
        injected = (incoming.astype(jnp.float32) + injected_row.astype(jnp.float32)).astype(
            jnp.bfloat16
        )
        entering = is_live & (section_index == 0)
        current = jnp.where(entering, injected, hidden_state)
        assign = lax.dynamic_slice(
            routes, (loop_round, 0, micro_idx, 0, 0), (1, 1, 1, tokens, 1)
        ).reshape(tokens)
        result = core_block(current, gain_row, router_rows, w_first, w_second, assign)
        return jnp.where(is_live, result, hidden_state)

    def advance_one(moment, hidden_state):
        arrived = shifted(hidden_state, "section", 1)
        return advance(moment, arrived)

    hidden_state = jnp.zeros(init_state.shape[1:], jnp.bfloat16)
    hidden_state = advance(0, hidden_state)
    hidden_state = lax.fori_loop(1, total_steps, advance_one, hidden_state)
    return hidden_state[None]


def solution(mesh):
    return jax.shard_map(
        body,
        mesh=mesh,
        in_specs=(
            P(None, ("dp", "expert"), None),
            P(None, ("dp", "expert"), None),
            P(None, "section", None, ("dp", "expert"), None),
            P("section", None),
            P("section", None, None),
            P("section", "expert", "dp", None),
            P("section", "expert", None, "dp"),
        ),
        out_specs=P("section", ("dp", "expert"), None),
        check_vma=False,
    )
```

```python
import jax
import jax.numpy as jnp
from jax import lax
from jax.sharding import PartitionSpec as P

RECUR = 2
CAP = 12


def shifted(block, axis, distance):
    devices = range(lax.axis_size(axis))
    route = [((i - distance) % len(devices), i) for i in devices]
    return lax.ppermute(block, axis, route)


def normalize(current, gain_row):
    as_float = current.astype(jnp.float32)
    inv_rms = lax.rsqrt(jnp.mean(as_float * as_float, axis=-1, keepdims=True) + 1e-05)
    return (as_float * inv_rms * gain_row).astype(jnp.bfloat16)


def expert_rows(item_rows, w_first, w_second):
    extent = item_rows.shape
    flat_rows = item_rows.reshape(-1, extent[-1])
    hidden = jax.nn.gelu(jnp.dot(flat_rows, w_first, preferred_element_type=jnp.float32)).astype(
        jnp.bfloat16
    )
    result = lax.dot_general(
        hidden, w_second, (((1,), (1,)), ((), ())), preferred_element_type=jnp.float32
    ).astype(jnp.bfloat16)
    return result.reshape(extent)


def whole_round(buffer, w_first, w_second):
    groups = buffer.shape[0]
    arrived = jnp.stack([buffer[0]] + [shifted(buffer[j], "expert", j) for j in range(1, groups)])
    processed = expert_rows(arrived, w_first, w_second)
    return jnp.stack(
        [processed[0]] + [shifted(processed[j], "expert", groups - j) for j in range(1, groups)]
    )


def core_block(current, gain_row, router_rows, w_first, w_second, assign):
    tokens = current.shape[0]
    experts = router_rows.shape[0]
    normed = normalize(current, gain_row)
    logits = jnp.dot(normed, router_rows.T, preferred_element_type=jnp.float32)
    labels = lax.broadcasted_iota(jnp.int32, (tokens, experts), 1)
    onehot = (assign[:, None] == labels).astype(jnp.float32)
    gate_value = jax.nn.sigmoid(jnp.sum(onehot * logits, axis=-1))
    earlier = (
        lax.broadcasted_iota(jnp.int32, (tokens, tokens), 0)
        > lax.broadcasted_iota(jnp.int32, (tokens, tokens), 1)
    ).astype(jnp.float32)
    counts = jnp.dot(earlier, onehot, preferred_element_type=jnp.float32)
    slot_index = jnp.sum(onehot * counts, axis=-1).astype(jnp.int32)
    relative = jnp.mod(assign - lax.axis_index("expert"), experts)
    target = relative * CAP + slot_index
    places = (
        lax.broadcasted_iota(jnp.int32, (experts * CAP, tokens), 0) == target[None, :]
    ).astype(jnp.bfloat16)
    buffer = (
        jnp.dot(places, normed, preferred_element_type=jnp.float32)
        .astype(jnp.bfloat16)
        .reshape(experts, CAP, -1)
    )
    returned = whole_round(buffer, w_first, w_second)
    flat_back = returned.reshape(experts * CAP, -1)
    expert_out = jnp.einsum("st,sd->td", places, flat_back, preferred_element_type=jnp.float32)
    updated = current.astype(jnp.float32) + gate_value[:, None] * expert_out
    return updated.astype(jnp.bfloat16)


def body(init_state, inject, routes, norm_gain, router, w_up, w_down):
    sections = lax.axis_size("section")
    section_index = lax.axis_index("section")
    up_all, down_all = (
        lax.all_gather(w_up, "dp", axis=2, tiled=True),
        lax.all_gather(jnp.swapaxes(w_down, 2, 3), "dp", axis=2, tiled=True),
    )
    w_first = up_all[0, 0]
    w_second = down_all[0, 0]
    gain_row = norm_gain[0]
    router_rows = router[0]
    tokens = init_state.shape[1]
    active_span = sections * RECUR
    total_steps = active_span + sections - 1

    def advance(moment, hidden_state):
        offset = moment - section_index
        is_live = (offset >= 0) & (offset < active_span)
        clipped = jnp.clip(offset, 0, active_span - 1)
        loop_round = clipped // sections
        entry_slot = clipped % sections
        micro_idx = jnp.mod(sections - 2 - entry_slot, sections)
        initial = lax.dynamic_index_in_dim(init_state, micro_idx, 0, keepdims=False)
        injected_row = lax.dynamic_index_in_dim(inject, micro_idx, 0, keepdims=False)
        incoming = jnp.where(loop_round == 0, initial, hidden_state)
        injected = (incoming.astype(jnp.float32) + injected_row.astype(jnp.float32)).astype(
            jnp.bfloat16
        )
        entering = is_live & (section_index == 0)
        current = jnp.where(entering, injected, hidden_state)
        assign = lax.dynamic_slice(
            routes, (loop_round, 0, micro_idx, 0, 0), (1, 1, 1, tokens, 1)
        ).reshape(tokens)
        result = core_block(current, gain_row, router_rows, w_first, w_second, assign)
        return jnp.where(is_live, result, hidden_state)

    def advance_one(moment, hidden_state):
        arrived = shifted(hidden_state, "section", 1)
        return advance(moment, arrived)

    hidden_state = jnp.zeros(init_state.shape[1:], jnp.bfloat16)
    hidden_state = advance(0, hidden_state)
    hidden_state = lax.fori_loop(1, total_steps, advance_one, hidden_state)
    return hidden_state[None]


def solution(mesh):
    return jax.shard_map(
        body,
        mesh=mesh,
        in_specs=(
            P(None, ("dp", "expert"), None),
            P(None, ("dp", "expert"), None),
            P(None, "section", None, ("dp", "expert"), None),
            P("section", None),
            P("section", None, None),
            P("section", "expert", "dp", None),
            P("section", "expert", None, "dp"),
        ),
        out_specs=P("section", ("dp", "expert"), None),
        check_vma=False,
    )
```

```python
import jax
import jax.numpy as jnp
from jax import lax
from jax.sharding import PartitionSpec as P

RECUR = 2
CAP = 12


def shifted(block, axis, distance):
    devices = range(lax.axis_size(axis))
    route = [((i - distance) % len(devices), i) for i in devices]
    return lax.ppermute(block, axis, route)


def normalize(current, gain_row):
    as_float = current.astype(jnp.float32)
    inv_rms = lax.rsqrt(jnp.mean(as_float * as_float, axis=-1, keepdims=True) + 1e-05)
    return (as_float * inv_rms * gain_row).astype(jnp.bfloat16)


def expert_rows(item_rows, w_first, w_second):
    extent = item_rows.shape
    flat_rows = item_rows.reshape(-1, extent[-1])
    hidden = jax.nn.gelu(jnp.dot(flat_rows, w_first, preferred_element_type=jnp.float32)).astype(
        jnp.bfloat16
    )
    result = lax.dot_general(
        hidden, w_second, (((1,), (1,)), ((), ())), preferred_element_type=jnp.float32
    ).astype(jnp.bfloat16)
    return result.reshape(extent)


def onward(block, distance):
    sections = lax.axis_size("section")
    experts = lax.axis_size("expert")
    route = [
        (s * experts + e, ((s + 1) % sections) * experts + (e - distance) % experts)
        for s in range(sections)
        for e in range(experts)
    ]
    return lax.ppermute(block, ("section", "expert"), route)


def core_block(current, gain_row, router_rows, w_first, w_second, assign):
    tokens = current.shape[0]
    experts = router_rows.shape[0]
    normed = normalize(current, gain_row)
    logits = jnp.dot(normed, router_rows.T, preferred_element_type=jnp.float32)
    labels = lax.broadcasted_iota(jnp.int32, (tokens, experts), 1)
    onehot = (assign[:, None] == labels).astype(jnp.float32)
    gate_value = jax.nn.sigmoid(jnp.sum(onehot * logits, axis=-1))
    earlier = (
        lax.broadcasted_iota(jnp.int32, (tokens, tokens), 0)
        > lax.broadcasted_iota(jnp.int32, (tokens, tokens), 1)
    ).astype(jnp.float32)
    counts = jnp.dot(earlier, onehot, preferred_element_type=jnp.float32)
    slot_index = jnp.sum(onehot * counts, axis=-1).astype(jnp.int32)
    relative = jnp.mod(assign - lax.axis_index("expert"), experts)
    target = relative * CAP + slot_index
    places = (
        lax.broadcasted_iota(jnp.int32, (experts * CAP, tokens), 0) == target[None, :]
    ).astype(jnp.bfloat16)
    buffer = (
        jnp.dot(places, normed, preferred_element_type=jnp.float32)
        .astype(jnp.bfloat16)
        .reshape(experts, CAP, -1)
    )
    arrived = jnp.stack([buffer[0]] + [shifted(buffer[j], "expert", j) for j in range(1, experts)])
    processed = expert_rows(arrived, w_first, w_second)
    back = jnp.stack([onward(processed[j], j) for j in range(experts)])
    return (
        shifted(current, "section", 1),
        shifted(gate_value, "section", 1),
        shifted(places, "section", 1),
        back,
    )


def combine(carry, was_live):
    kept, gate_value, places, back = carry
    flat_back = back.reshape(-1, back.shape[-1])
    expert_out = jnp.einsum("st,sd->td", places, flat_back, preferred_element_type=jnp.float32)
    updated = (kept.astype(jnp.float32) + gate_value[:, None] * expert_out).astype(jnp.bfloat16)
    return jnp.where(was_live, updated, kept)


def body(init_state, inject, routes, norm_gain, router, w_up, w_down):
    sections = lax.axis_size("section")
    section_index = lax.axis_index("section")
    up_all, down_all = (
        lax.all_gather(w_up, "dp", axis=2, tiled=True),
        lax.all_gather(jnp.swapaxes(w_down, 2, 3), "dp", axis=2, tiled=True),
    )
    w_first = up_all[0, 0]
    w_second = down_all[0, 0]
    gain_row = norm_gain[0]
    router_rows = router[0]
    tokens = init_state.shape[1]
    active_span = sections * RECUR
    total_steps = active_span + sections - 1
    previous_section = jnp.mod(section_index - 1, sections)

    def live_at(moment, section):
        offset = moment - section
        return (offset >= 0) & (offset < active_span)

    def advance(moment, hidden_state):
        offset = moment - section_index
        is_live = live_at(moment, section_index)
        clipped = jnp.clip(offset, 0, active_span - 1)
        loop_round = clipped // sections
        entry_slot = clipped % sections
        micro_idx = jnp.mod(sections - 1 - entry_slot, sections)
        initial = lax.dynamic_index_in_dim(init_state, micro_idx, 0, keepdims=False)
        injected_row = lax.dynamic_index_in_dim(inject, micro_idx, 0, keepdims=False)
        incoming = jnp.where(loop_round == 0, initial, hidden_state)
        injected = (incoming.astype(jnp.float32) + injected_row.astype(jnp.float32)).astype(
            jnp.bfloat16
        )
        entering = is_live & (section_index == 0)
        current = jnp.where(entering, injected, hidden_state)
        assign = lax.dynamic_slice(
            routes, (loop_round, 0, micro_idx, 0, 0), (1, 1, 1, tokens, 1)
        ).reshape(tokens)
        return core_block(current, gain_row, router_rows, w_first, w_second, assign)

    def advance_one(moment, carry):
        arrived = combine(carry, live_at(moment - 1, previous_section))
        return advance(moment, arrived)

    carry = advance(0, jnp.zeros(init_state.shape[1:], jnp.bfloat16))
    carry = lax.fori_loop(1, total_steps, advance_one, carry)
    final = combine(carry, live_at(total_steps - 1, previous_section))
    return final[None]


def solution(mesh):
    return jax.shard_map(
        body,
        mesh=mesh,
        in_specs=(
            P(None, ("dp", "expert"), None),
            P(None, ("dp", "expert"), None),
            P(None, "section", None, ("dp", "expert"), None),
            P("section", None),
            P("section", None, None),
            P("section", "expert", "dp", None),
            P("section", "expert", None, "dp"),
        ),
        out_specs=P("section", ("dp", "expert"), None),
        check_vma=False,
    )
```

```python
import functools

import jax
import jax.numpy as jnp
from jax import lax
from jax.experimental import pallas as pl
from jax.experimental.pallas import tpu as pltpu
from jax.sharding import PartitionSpec as P

MESH = pl.DeviceIdType.MESH
SLAB = 16

RECUR = 2
CAP = 12


def shifted(block, axis, distance):
    devices = range(lax.axis_size(axis))
    route = [((i - distance) % len(devices), i) for i in devices]
    return lax.ppermute(block, axis, route)


def normalize(current, gain_row):
    as_float = current.astype(jnp.float32)
    inv_rms = lax.rsqrt(jnp.mean(as_float * as_float, axis=-1, keepdims=True) + 1e-05)
    return (as_float * inv_rms * gain_row).astype(jnp.bfloat16)


def expert_rows(item_rows, w_first, w_second):
    extent = item_rows.shape
    flat_rows = item_rows.reshape(-1, extent[-1])
    hidden = jax.nn.gelu(jnp.dot(flat_rows, w_first, preferred_element_type=jnp.float32)).astype(
        jnp.bfloat16
    )
    result = lax.dot_general(
        hidden, w_second, (((1,), (1,)), ((), ())), preferred_element_type=jnp.float32
    ).astype(jnp.bfloat16)
    return result.reshape(extent)


def exchange_kernel(direction, src_ref, dst_ref, send_sem, recv_sem):
    groups = src_ref.shape[0]
    me = lax.axis_index("expert")
    place = (lax.axis_index("section"), lax.axis_index("dp"))
    barrier = pltpu.get_barrier_semaphore()
    for j in range(1, groups):
        pl.semaphore_signal(
            barrier, inc=1, device_id=place + (lax.rem(me + j, groups),), device_id_type=MESH
        )
    pl.semaphore_wait(barrier, groups - 1)
    copies = []
    for j in range(1, groups):
        copy = pltpu.make_async_remote_copy(
            src_ref=src_ref.at[j],
            dst_ref=dst_ref.at[j],
            send_sem=send_sem.at[j - 1],
            recv_sem=recv_sem.at[j - 1],
            device_id=place + (lax.rem(me + direction * j + groups, groups),),
            device_id_type=MESH,
        )
        copy.start()
        copies.append(copy)
    dst_ref[0] = src_ref[0]
    for copy in copies:
        copy.wait()


def exchange(buffer, direction, channel):
    groups = buffer.shape[0]
    return pl.pallas_call(
        functools.partial(exchange_kernel, direction),
        out_shape=jax.ShapeDtypeStruct(buffer.shape, buffer.dtype),
        in_specs=[pl.BlockSpec(memory_space=pltpu.VMEM)],
        out_specs=pl.BlockSpec(memory_space=pltpu.VMEM),
        scratch_shapes=[
            pltpu.SemaphoreType.DMA((groups - 1,)),
            pltpu.SemaphoreType.DMA((groups - 1,)),
        ],
        compiler_params=pltpu.CompilerParams(collective_id=channel, has_side_effects=True),
    )(buffer)


def whole_round(buffer, w_first, w_second):
    arrived = exchange(buffer, 1, 0)
    processed = expert_rows(arrived, w_first, w_second)
    return exchange(processed, -1, 1)


def core_block(current, gain_row, router_rows, w_first, w_second, assign):
    tokens = current.shape[0]
    experts = router_rows.shape[0]
    normed = normalize(current, gain_row)
    logits = jnp.dot(normed, router_rows.T, preferred_element_type=jnp.float32)
    labels = lax.broadcasted_iota(jnp.int32, (tokens, experts), 1)
    onehot = (assign[:, None] == labels).astype(jnp.float32)
    gate_value = jax.nn.sigmoid(jnp.sum(onehot * logits, axis=-1))
    earlier = (
        lax.broadcasted_iota(jnp.int32, (tokens, tokens), 0)
        > lax.broadcasted_iota(jnp.int32, (tokens, tokens), 1)
    ).astype(jnp.float32)
    counts = jnp.dot(earlier, onehot, preferred_element_type=jnp.float32)
    slot_index = jnp.sum(onehot * counts, axis=-1).astype(jnp.int32)
    relative = jnp.mod(assign - lax.axis_index("expert"), experts)
    target = relative * SLAB + slot_index
    places = (
        lax.broadcasted_iota(jnp.int32, (experts * SLAB, tokens), 0) == target[None, :]
    ).astype(jnp.bfloat16)
    buffer = (
        jnp.dot(places, normed, preferred_element_type=jnp.float32)
        .astype(jnp.bfloat16)
        .reshape(experts, SLAB, -1)
    )
    returned = whole_round(buffer, w_first, w_second)
    flat_back = returned.reshape(experts * SLAB, -1)
    expert_out = jnp.einsum("st,sd->td", places, flat_back, preferred_element_type=jnp.float32)
    updated = current.astype(jnp.float32) + gate_value[:, None] * expert_out
    return updated.astype(jnp.bfloat16)


def body(init_state, inject, routes, norm_gain, router, w_up, w_down):
    sections = lax.axis_size("section")
    section_index = lax.axis_index("section")
    up_all, down_all = (
        lax.all_gather(w_up, "dp", axis=2, tiled=True),
        lax.all_gather(jnp.swapaxes(w_down, 2, 3), "dp", axis=2, tiled=True),
    )
    w_first = up_all[0, 0]
    w_second = down_all[0, 0]
    gain_row = norm_gain[0]
    router_rows = router[0]
    tokens = init_state.shape[1]
    active_span = sections * RECUR
    total_steps = active_span + sections - 1

    def advance(moment, hidden_state):
        offset = moment - section_index
        is_live = (offset >= 0) & (offset < active_span)
        clipped = jnp.clip(offset, 0, active_span - 1)
        loop_round = clipped // sections
        entry_slot = clipped % sections
        micro_idx = jnp.mod(sections - 2 - entry_slot, sections)
        initial = lax.dynamic_index_in_dim(init_state, micro_idx, 0, keepdims=False)
        injected_row = lax.dynamic_index_in_dim(inject, micro_idx, 0, keepdims=False)
        incoming = jnp.where(loop_round == 0, initial, hidden_state)
        injected = (incoming.astype(jnp.float32) + injected_row.astype(jnp.float32)).astype(
            jnp.bfloat16
        )
        entering = is_live & (section_index == 0)
        current = jnp.where(entering, injected, hidden_state)
        assign = lax.dynamic_slice(
            routes, (loop_round, 0, micro_idx, 0, 0), (1, 1, 1, tokens, 1)
        ).reshape(tokens)
        result = core_block(current, gain_row, router_rows, w_first, w_second, assign)
        return jnp.where(is_live, result, hidden_state)

    def advance_one(moment, hidden_state):
        arrived = shifted(hidden_state, "section", 1)
        return advance(moment, arrived)

    hidden_state = jnp.zeros(init_state.shape[1:], jnp.bfloat16)
    hidden_state = advance(0, hidden_state)
    hidden_state = lax.fori_loop(1, total_steps, advance_one, hidden_state)
    return hidden_state[None]


def solution(mesh):
    return jax.shard_map(
        body,
        mesh=mesh,
        in_specs=(
            P(None, ("dp", "expert"), None),
            P(None, ("dp", "expert"), None),
            P(None, "section", None, ("dp", "expert"), None),
            P("section", None),
            P("section", None, None),
            P("section", "expert", "dp", None),
            P("section", "expert", None, "dp"),
        ),
        out_specs=P("section", ("dp", "expert"), None),
        check_vma=False,
    )
```

```python
import functools

import jax
import jax.numpy as jnp
from jax import lax
from jax.experimental import pallas as pl
from jax.experimental.pallas import tpu as pltpu
from jax.sharding import PartitionSpec as P

CHUNK = 256

RECUR = 2
CAP = 12


def shifted(block, axis, distance):
    devices = range(lax.axis_size(axis))
    route = [((i - distance) % len(devices), i) for i in devices]
    return lax.ppermute(block, axis, route)


def normalize(current, gain_row):
    as_float = current.astype(jnp.float32)
    inv_rms = lax.rsqrt(jnp.mean(as_float * as_float, axis=-1, keepdims=True) + 1e-05)
    return (as_float * inv_rms * gain_row).astype(jnp.bfloat16)


def mlp_kernel(rows_ref, up_ref, down_ref, out_ref, total_ref):
    step = pl.program_id(0)

    @pl.when(step == 0)
    def _():
        total_ref[...] = jnp.zeros_like(total_ref)

    hidden = jax.nn.gelu(
        jnp.dot(rows_ref[...], up_ref[...], preferred_element_type=jnp.float32)
    ).astype(jnp.bfloat16)
    total_ref[...] += lax.dot_general(
        hidden, down_ref[...], (((1,), (1,)), ((), ())), preferred_element_type=jnp.float32
    )

    @pl.when(step == pl.num_programs(0) - 1)
    def _():
        out_ref[...] = total_ref[...].astype(out_ref.dtype)


def expert_rows(item_rows, w_first, w_second):
    extent = item_rows.shape
    flat_rows = item_rows.reshape(-1, extent[-1])
    count, width = flat_rows.shape
    inner = w_first.shape[1]
    result = pl.pallas_call(
        mlp_kernel,
        out_shape=jax.ShapeDtypeStruct((count, width), jnp.bfloat16),
        grid=(inner // CHUNK,),
        in_specs=[
            pl.BlockSpec((count, width), lambda k: (0, 0)),
            pl.BlockSpec((width, CHUNK), lambda k: (0, k)),
            pl.BlockSpec((width, CHUNK), lambda k: (0, k)),
        ],
        out_specs=pl.BlockSpec((count, width), lambda k: (0, 0)),
        scratch_shapes=[pltpu.VMEM((count, width), jnp.float32)],
        compiler_params=pltpu.CompilerParams(dimension_semantics=("arbitrary",)),
        cost_estimate=pl.CostEstimate(
            flops=4 * count * width * inner,
            bytes_accessed=2 * (2 * width * inner + 2 * count * width),
            transcendentals=count * inner,
        ),
    )(flat_rows, w_first, w_second)
    return result.reshape(extent)


def whole_round(buffer, w_first, w_second):
    groups = buffer.shape[0]
    arrived = jnp.stack([buffer[0]] + [shifted(buffer[j], "expert", j) for j in range(1, groups)])
    processed = expert_rows(arrived, w_first, w_second)
    return jnp.stack(
        [processed[0]] + [shifted(processed[j], "expert", groups - j) for j in range(1, groups)]
    )


def core_block(current, gain_row, router_rows, w_first, w_second, assign):
    tokens = current.shape[0]
    experts = router_rows.shape[0]
    normed = normalize(current, gain_row)
    logits = jnp.dot(normed, router_rows.T, preferred_element_type=jnp.float32)
    labels = lax.broadcasted_iota(jnp.int32, (tokens, experts), 1)
    onehot = (assign[:, None] == labels).astype(jnp.float32)
    gate_value = jax.nn.sigmoid(jnp.sum(onehot * logits, axis=-1))
    earlier = (
        lax.broadcasted_iota(jnp.int32, (tokens, tokens), 0)
        > lax.broadcasted_iota(jnp.int32, (tokens, tokens), 1)
    ).astype(jnp.float32)
    counts = jnp.dot(earlier, onehot, preferred_element_type=jnp.float32)
    slot_index = jnp.sum(onehot * counts, axis=-1).astype(jnp.int32)
    relative = jnp.mod(assign - lax.axis_index("expert"), experts)
    target = relative * CAP + slot_index
    places = (
        lax.broadcasted_iota(jnp.int32, (experts * CAP, tokens), 0) == target[None, :]
    ).astype(jnp.bfloat16)
    buffer = (
        jnp.dot(places, normed, preferred_element_type=jnp.float32)
        .astype(jnp.bfloat16)
        .reshape(experts, CAP, -1)
    )
    returned = whole_round(buffer, w_first, w_second)
    flat_back = returned.reshape(experts * CAP, -1)
    expert_out = jnp.einsum("st,sd->td", places, flat_back, preferred_element_type=jnp.float32)
    updated = current.astype(jnp.float32) + gate_value[:, None] * expert_out
    return updated.astype(jnp.bfloat16)


def body(init_state, inject, routes, norm_gain, router, w_up, w_down):
    sections = lax.axis_size("section")
    section_index = lax.axis_index("section")
    up_all, down_all = (
        lax.all_gather(w_up, "dp", axis=2, tiled=True),
        lax.all_gather(jnp.swapaxes(w_down, 2, 3), "dp", axis=2, tiled=True),
    )
    w_first = up_all[0, 0]
    w_second = down_all[0, 0]
    gain_row = norm_gain[0]
    router_rows = router[0]
    tokens = init_state.shape[1]
    active_span = sections * RECUR
    total_steps = active_span + sections - 1

    def advance(moment, hidden_state):
        offset = moment - section_index
        is_live = (offset >= 0) & (offset < active_span)
        clipped = jnp.clip(offset, 0, active_span - 1)
        loop_round = clipped // sections
        entry_slot = clipped % sections
        micro_idx = jnp.mod(sections - 2 - entry_slot, sections)
        initial = lax.dynamic_index_in_dim(init_state, micro_idx, 0, keepdims=False)
        injected_row = lax.dynamic_index_in_dim(inject, micro_idx, 0, keepdims=False)
        incoming = jnp.where(loop_round == 0, initial, hidden_state)
        injected = (incoming.astype(jnp.float32) + injected_row.astype(jnp.float32)).astype(
            jnp.bfloat16
        )
        entering = is_live & (section_index == 0)
        current = jnp.where(entering, injected, hidden_state)
        assign = lax.dynamic_slice(
            routes, (loop_round, 0, micro_idx, 0, 0), (1, 1, 1, tokens, 1)
        ).reshape(tokens)
        result = core_block(current, gain_row, router_rows, w_first, w_second, assign)
        return jnp.where(is_live, result, hidden_state)

    def advance_one(moment, hidden_state):
        arrived = shifted(hidden_state, "section", 1)
        return advance(moment, arrived)

    hidden_state = jnp.zeros(init_state.shape[1:], jnp.bfloat16)
    hidden_state = advance(0, hidden_state)
    hidden_state = lax.fori_loop(1, total_steps, advance_one, hidden_state)
    return hidden_state[None]


def solution(mesh):
    return jax.shard_map(
        body,
        mesh=mesh,
        in_specs=(
            P(None, ("dp", "expert"), None),
            P(None, ("dp", "expert"), None),
            P(None, "section", None, ("dp", "expert"), None),
            P("section", None),
            P("section", None, None),
            P("section", "expert", "dp", None),
            P("section", "expert", None, "dp"),
        ),
        out_specs=P("section", ("dp", "expert"), None),
        check_vma=False,
    )
```

```python
import jax
import jax.numpy as jnp
from jax import lax
from jax.sharding import PartitionSpec as P

RECUR = 2
CAP = 12


def shifted(block, axis, distance):
    devices = range(lax.axis_size(axis))
    route = [((i - distance) % len(devices), i) for i in devices]
    return lax.ppermute(block, axis, route)


def doubling_gather(piece, axis):
    count = lax.axis_size(axis)
    me = lax.axis_index(axis)
    held = piece
    bit = count // 2
    while bit >= 1:
        theirs = lax.ppermute(held, axis, [(i, i ^ bit) for i in range(count)])
        upper = (me & bit) != 0
        held = jnp.stack([jnp.where(upper, theirs, held), jnp.where(upper, held, theirs)])
        bit //= 2
    rank = held.ndim - piece.ndim
    order = tuple(reversed(range(rank))) + tuple(range(rank, held.ndim))
    held = jnp.transpose(held, order)
    return held.reshape((count * piece.shape[0],) + piece.shape[1:])


def normalize(current, gain_row):
    as_float = current.astype(jnp.float32)
    inv_rms = lax.rsqrt(jnp.mean(as_float * as_float, axis=-1, keepdims=True) + 1e-05)
    return (as_float * inv_rms * gain_row).astype(jnp.bfloat16)


def expert_rows(item_rows, w_first, w_second):
    extent = item_rows.shape
    flat_rows = item_rows.reshape(-1, extent[-1])
    hidden = jax.nn.gelu(jnp.dot(flat_rows, w_first, preferred_element_type=jnp.float32)).astype(
        jnp.bfloat16
    )
    result = lax.dot_general(
        hidden, w_second, (((1,), (1,)), ((), ())), preferred_element_type=jnp.float32
    ).astype(jnp.bfloat16)
    return result.reshape(extent)


def whole_round(buffer, w_first, w_second):
    groups = buffer.shape[0]
    arrived = jnp.stack([buffer[0]] + [shifted(buffer[j], "expert", j) for j in range(1, groups)])
    processed = expert_rows(arrived, w_first, w_second)
    return jnp.stack(
        [processed[0]] + [shifted(processed[j], "expert", groups - j) for j in range(1, groups)]
    )


def core_block(current, gain_row, router_rows, w_first, w_second, assign):
    tokens = current.shape[0]
    experts = router_rows.shape[0]
    normed = normalize(current, gain_row)
    logits = jnp.dot(normed, router_rows.T, preferred_element_type=jnp.float32)
    labels = lax.broadcasted_iota(jnp.int32, (tokens, experts), 1)
    onehot = (assign[:, None] == labels).astype(jnp.float32)
    gate_value = jax.nn.sigmoid(jnp.sum(onehot * logits, axis=-1))
    earlier = (
        lax.broadcasted_iota(jnp.int32, (tokens, tokens), 0)
        > lax.broadcasted_iota(jnp.int32, (tokens, tokens), 1)
    ).astype(jnp.float32)
    counts = jnp.dot(earlier, onehot, preferred_element_type=jnp.float32)
    slot_index = jnp.sum(onehot * counts, axis=-1).astype(jnp.int32)
    relative = jnp.mod(assign - lax.axis_index("expert"), experts)
    target = relative * CAP + slot_index
    places = (
        lax.broadcasted_iota(jnp.int32, (experts * CAP, tokens), 0) == target[None, :]
    ).astype(jnp.bfloat16)
    buffer = (
        jnp.dot(places, normed, preferred_element_type=jnp.float32)
        .astype(jnp.bfloat16)
        .reshape(experts, CAP, -1)
    )
    returned = whole_round(buffer, w_first, w_second)
    flat_back = returned.reshape(experts * CAP, -1)
    expert_out = jnp.einsum("st,sd->td", places, flat_back, preferred_element_type=jnp.float32)
    updated = current.astype(jnp.float32) + gate_value[:, None] * expert_out
    return updated.astype(jnp.bfloat16)


def body(init_state, inject, routes, norm_gain, router, w_up, w_down):
    sections = lax.axis_size("section")
    section_index = lax.axis_index("section")
    up_all = lax.all_gather(w_up, "dp", axis=2, tiled=True)
    w_first = up_all[0, 0]
    w_second = doubling_gather(jnp.swapaxes(w_down[0, 0], 0, 1), "dp")
    gain_row = norm_gain[0]
    router_rows = router[0]
    tokens = init_state.shape[1]
    active_span = sections * RECUR
    total_steps = active_span + sections - 1

    def advance(moment, hidden_state):
        offset = moment - section_index
        is_live = (offset >= 0) & (offset < active_span)
        clipped = jnp.clip(offset, 0, active_span - 1)
        loop_round = clipped // sections
        entry_slot = clipped % sections
        micro_idx = jnp.mod(sections - 2 - entry_slot, sections)
        initial = lax.dynamic_index_in_dim(init_state, micro_idx, 0, keepdims=False)
        injected_row = lax.dynamic_index_in_dim(inject, micro_idx, 0, keepdims=False)
        incoming = jnp.where(loop_round == 0, initial, hidden_state)
        injected = (incoming.astype(jnp.float32) + injected_row.astype(jnp.float32)).astype(
            jnp.bfloat16
        )
        entering = is_live & (section_index == 0)
        current = jnp.where(entering, injected, hidden_state)
        assign = lax.dynamic_slice(
            routes, (loop_round, 0, micro_idx, 0, 0), (1, 1, 1, tokens, 1)
        ).reshape(tokens)
        result = core_block(current, gain_row, router_rows, w_first, w_second, assign)
        return jnp.where(is_live, result, hidden_state)

    def advance_one(moment, hidden_state):
        arrived = shifted(hidden_state, "section", 1)
        return advance(moment, arrived)

    hidden_state = jnp.zeros(init_state.shape[1:], jnp.bfloat16)
    hidden_state = advance(0, hidden_state)
    hidden_state = lax.fori_loop(1, total_steps, advance_one, hidden_state)
    return hidden_state[None]


def solution(mesh):
    return jax.shard_map(
        body,
        mesh=mesh,
        in_specs=(
            P(None, ("dp", "expert"), None),
            P(None, ("dp", "expert"), None),
            P(None, "section", None, ("dp", "expert"), None),
            P("section", None),
            P("section", None, None),
            P("section", "expert", "dp", None),
            P("section", "expert", None, "dp"),
        ),
        out_specs=P("section", ("dp", "expert"), None),
        check_vma=False,
    )
```

```python
import jax
import jax.numpy as jnp
from jax import lax
from jax.sharding import PartitionSpec as P

RECUR = 2
CAP = 12


def shifted(block, axis, distance):
    devices = range(lax.axis_size(axis))
    route = [((i - distance) % len(devices), i) for i in devices]
    return lax.ppermute(block, axis, route)


def normalize(current, gain_row):
    as_float = current.astype(jnp.float32)
    inv_rms = lax.rsqrt(jnp.mean(as_float * as_float, axis=-1, keepdims=True) + 1e-05)
    return (as_float * inv_rms * gain_row).astype(jnp.bfloat16)


def expert_rows(item_rows, w_first, w_second):
    extent = item_rows.shape
    flat_rows = item_rows.reshape(-1, extent[-1])
    hidden = jax.nn.gelu(jnp.dot(flat_rows, w_first, preferred_element_type=jnp.float32)).astype(
        jnp.bfloat16
    )
    result = lax.dot_general(
        hidden, w_second, (((1,), (1,)), ((), ())), preferred_element_type=jnp.float32
    ).astype(jnp.bfloat16)
    return result.reshape(extent)


def onward(block, distance):
    sections = lax.axis_size("section")
    experts = lax.axis_size("expert")
    route = [
        (s * experts + e, ((s + 1) % sections) * experts + (e - distance) % experts)
        for s in range(sections)
        for e in range(experts)
    ]
    return lax.ppermute(block, ("section", "expert"), route)


def front(current, gain_row, router_rows, assign):
    tokens = current.shape[0]
    experts = router_rows.shape[0]
    normed = normalize(current, gain_row)
    logits = jnp.dot(normed, router_rows.T, preferred_element_type=jnp.float32)
    labels = lax.broadcasted_iota(jnp.int32, (tokens, experts), 1)
    onehot = (assign[:, None] == labels).astype(jnp.float32)
    gate_value = jax.nn.sigmoid(jnp.sum(onehot * logits, axis=-1))
    earlier = (
        lax.broadcasted_iota(jnp.int32, (tokens, tokens), 0)
        > lax.broadcasted_iota(jnp.int32, (tokens, tokens), 1)
    ).astype(jnp.float32)
    counts = jnp.dot(earlier, onehot, preferred_element_type=jnp.float32)
    slot_index = jnp.sum(onehot * counts, axis=-1).astype(jnp.int32)
    relative = jnp.mod(assign - lax.axis_index("expert"), experts)
    target = relative * CAP + slot_index
    places = (
        lax.broadcasted_iota(jnp.int32, (experts * CAP, tokens), 0) == target[None, :]
    ).astype(jnp.bfloat16)
    return normed, gate_value, places


def core_block(current, gain_row, router_rows, w_first, w_second, assign):
    experts = router_rows.shape[0]
    normed, _, places = front(current, gain_row, router_rows, assign)
    buffer = (
        jnp.dot(places, normed, preferred_element_type=jnp.float32)
        .astype(jnp.bfloat16)
        .reshape(experts, CAP, -1)
    )
    arrived = jnp.stack([buffer[0]] + [shifted(buffer[j], "expert", j) for j in range(1, experts)])
    processed = expert_rows(arrived, w_first, w_second)
    packed = onward(jnp.concatenate([processed[0], current]), 0)
    return (packed,) + tuple(onward(processed[j], j) for j in range(1, experts))


def body(init_state, inject, routes, norm_gain, router, w_up, w_down):
    sections = lax.axis_size("section")
    section_index = lax.axis_index("section")
    up_all, down_all = (
        lax.all_gather(w_up, "dp", axis=2, tiled=True),
        lax.all_gather(jnp.swapaxes(w_down, 2, 3), "dp", axis=2, tiled=True),
    )
    gains = lax.all_gather(norm_gain, "section", axis=0, tiled=True)
    routers = lax.all_gather(router, "section", axis=0, tiled=True)
    all_routes = lax.all_gather(routes, "section", axis=1, tiled=True)
    w_first = up_all[0, 0]
    w_second = down_all[0, 0]
    tokens = init_state.shape[1]
    active_span = sections * RECUR
    total_steps = active_span + sections - 1
    previous_section = jnp.mod(section_index - 1, sections)

    def live_at(moment, section):
        offset = moment - section
        return (offset >= 0) & (offset < active_span)

    def schedule(moment, section):
        clipped = jnp.clip(moment - section, 0, active_span - 1)
        loop_round = clipped // sections
        micro_idx = jnp.mod(sections - 1 - clipped % sections, sections)
        assign = lax.dynamic_slice(
            all_routes, (loop_round, section, micro_idx, 0, 0), (1, 1, 1, tokens, 1)
        ).reshape(tokens)
        return loop_round, micro_idx, assign

    def combine(moment, carry):
        packed, *rest = carry
        slots = packed.shape[0] - tokens
        kept = packed[slots:]
        _, _, assign = schedule(moment - 1, previous_section)
        _, gate_value, places = front(
            kept,
            lax.dynamic_index_in_dim(gains, previous_section, 0, keepdims=False),
            lax.dynamic_index_in_dim(routers, previous_section, 0, keepdims=False),
            assign,
        )
        flat_back = jnp.concatenate([packed[:slots]] + list(rest))
        expert_out = jnp.einsum("st,sd->td", places, flat_back, preferred_element_type=jnp.float32)
        updated = (kept.astype(jnp.float32) + gate_value[:, None] * expert_out).astype(jnp.bfloat16)
        return jnp.where(live_at(moment - 1, previous_section), updated, kept)

    def advance(moment, hidden_state):
        is_live = live_at(moment, section_index)
        loop_round, micro_idx, assign = schedule(moment, section_index)
        initial = lax.dynamic_index_in_dim(init_state, micro_idx, 0, keepdims=False)
        injected_row = lax.dynamic_index_in_dim(inject, micro_idx, 0, keepdims=False)
        incoming = jnp.where(loop_round == 0, initial, hidden_state)
        injected = (incoming.astype(jnp.float32) + injected_row.astype(jnp.float32)).astype(
            jnp.bfloat16
        )
        entering = is_live & (section_index == 0)
        current = jnp.where(entering, injected, hidden_state)
        gain_row = lax.dynamic_index_in_dim(gains, section_index, 0, keepdims=False)
        router_rows = lax.dynamic_index_in_dim(routers, section_index, 0, keepdims=False)
        return core_block(current, gain_row, router_rows, w_first, w_second, assign)

    def advance_one(moment, carry):
        return advance(moment, combine(moment, carry))

    carry = advance(0, jnp.zeros(init_state.shape[1:], jnp.bfloat16))
    carry = lax.fori_loop(1, total_steps, advance_one, carry)
    return combine(total_steps, carry)[None]


def solution(mesh):
    return jax.shard_map(
        body,
        mesh=mesh,
        in_specs=(
            P(None, ("dp", "expert"), None),
            P(None, ("dp", "expert"), None),
            P(None, "section", None, ("dp", "expert"), None),
            P("section", None),
            P("section", None, None),
            P("section", "expert", "dp", None),
            P("section", "expert", None, "dp"),
        ),
        out_specs=P("section", ("dp", "expert"), None),
        check_vma=False,
    )
```

```python
import jax
import jax.numpy as jnp
from jax import lax
from jax.sharding import PartitionSpec as P

RECUR = 2
CAP = 12


def shifted(block, axis, distance):
    devices = range(lax.axis_size(axis))
    route = [((i - distance) % len(devices), i) for i in devices]
    return lax.ppermute(block, axis, route)


def normalize(current, gain_row):
    as_float = current.astype(jnp.float32)
    inv_rms = lax.rsqrt(jnp.mean(as_float * as_float, axis=-1, keepdims=True) + 1e-05)
    return (as_float * inv_rms * gain_row).astype(jnp.bfloat16)


def expert_rows(item_rows, w_first, w_second):
    extent = item_rows.shape
    flat_rows = item_rows.reshape(-1, extent[-1])
    hidden = jax.nn.gelu(jnp.dot(flat_rows, w_first, preferred_element_type=jnp.float32)).astype(
        jnp.bfloat16
    )
    result = lax.dot_general(
        hidden, w_second, (((1,), (1,)), ((), ())), preferred_element_type=jnp.float32
    ).astype(jnp.bfloat16)
    return result.reshape(extent)


def onward(block, distance):
    sections = lax.axis_size("section")
    experts = lax.axis_size("expert")
    route = [
        (s * experts + e, ((s + 1) % sections) * experts + (e - distance) % experts)
        for s in range(sections)
        for e in range(experts)
    ]
    return lax.ppermute(block, ("section", "expert"), route)


def front(current, gain_row, router_rows, assign):
    tokens = current.shape[0]
    experts = router_rows.shape[0]
    normed = normalize(current, gain_row)
    logits = jnp.dot(normed, router_rows.T, preferred_element_type=jnp.float32)
    labels = lax.broadcasted_iota(jnp.int32, (tokens, experts), 1)
    onehot = (assign[:, None] == labels).astype(jnp.float32)
    gate_value = jax.nn.sigmoid(jnp.sum(onehot * logits, axis=-1))
    earlier = (
        lax.broadcasted_iota(jnp.int32, (tokens, tokens), 0)
        > lax.broadcasted_iota(jnp.int32, (tokens, tokens), 1)
    ).astype(jnp.float32)
    counts = jnp.dot(earlier, onehot, preferred_element_type=jnp.float32)
    slot_index = jnp.sum(onehot * counts, axis=-1).astype(jnp.int32)
    relative = jnp.mod(assign - lax.axis_index("expert"), experts)
    target = relative * CAP + slot_index
    places = (
        lax.broadcasted_iota(jnp.int32, (experts * CAP, tokens), 0) == target[None, :]
    ).astype(jnp.bfloat16)
    return normed, gate_value, places


def core_block(current, gain_row, router_rows, w_first, w_second, assign):
    experts = router_rows.shape[0]
    normed, _, places = front(current, gain_row, router_rows, assign)
    buffer = (
        jnp.dot(places, normed, preferred_element_type=jnp.float32)
        .astype(jnp.bfloat16)
        .reshape(experts, CAP, -1)
    )
    arrived = jnp.stack([buffer[0]] + [shifted(buffer[j], "expert", j) for j in range(1, experts)])
    processed = expert_rows(arrived, w_first, w_second)
    packed = onward(jnp.concatenate([processed[0], current]), 0)
    return (packed,) + tuple(onward(processed[j], j) for j in range(1, experts))


def body(init_state, inject, routes, norm_gain, router, w_up, w_down):
    sections = lax.axis_size("section")
    section_index = lax.axis_index("section")
    rows = w_up.shape[2]
    pieces = jnp.concatenate([w_up[0, 0], jnp.swapaxes(w_down[0, 0], 0, 1)], axis=0)
    both = lax.all_gather(pieces, "dp", axis=0, tiled=False)
    gains = lax.all_gather(norm_gain, "section", axis=0, tiled=True)
    routers = lax.all_gather(router, "section", axis=0, tiled=True)
    all_routes = lax.all_gather(routes, "section", axis=1, tiled=True)
    w_first = both[:, :rows].reshape(-1, both.shape[-1])
    w_second = both[:, rows:].reshape(-1, both.shape[-1])
    tokens = init_state.shape[1]
    active_span = sections * RECUR
    total_steps = active_span + sections - 1
    previous_section = jnp.mod(section_index - 1, sections)

    def live_at(moment, section):
        offset = moment - section
        return (offset >= 0) & (offset < active_span)

    def schedule(moment, section):
        clipped = jnp.clip(moment - section, 0, active_span - 1)
        loop_round = clipped // sections
        micro_idx = jnp.mod(sections - 1 - clipped % sections, sections)
        assign = lax.dynamic_slice(
            all_routes, (loop_round, section, micro_idx, 0, 0), (1, 1, 1, tokens, 1)
        ).reshape(tokens)
        return loop_round, micro_idx, assign

    def combine(moment, carry):
        packed, *rest = carry
        slots = packed.shape[0] - tokens
        kept = packed[slots:]
        _, _, assign = schedule(moment - 1, previous_section)
        _, gate_value, places = front(
            kept,
            lax.dynamic_index_in_dim(gains, previous_section, 0, keepdims=False),
            lax.dynamic_index_in_dim(routers, previous_section, 0, keepdims=False),
            assign,
        )
        flat_back = jnp.concatenate([packed[:slots]] + list(rest))
        expert_out = jnp.einsum("st,sd->td", places, flat_back, preferred_element_type=jnp.float32)
        updated = (kept.astype(jnp.float32) + gate_value[:, None] * expert_out).astype(jnp.bfloat16)
        return jnp.where(live_at(moment - 1, previous_section), updated, kept)

    def advance(moment, hidden_state):
        is_live = live_at(moment, section_index)
        loop_round, micro_idx, assign = schedule(moment, section_index)
        initial = lax.dynamic_index_in_dim(init_state, micro_idx, 0, keepdims=False)
        injected_row = lax.dynamic_index_in_dim(inject, micro_idx, 0, keepdims=False)
        incoming = jnp.where(loop_round == 0, initial, hidden_state)
        injected = (incoming.astype(jnp.float32) + injected_row.astype(jnp.float32)).astype(
            jnp.bfloat16
        )
        entering = is_live & (section_index == 0)
        current = jnp.where(entering, injected, hidden_state)
        gain_row = lax.dynamic_index_in_dim(gains, section_index, 0, keepdims=False)
        router_rows = lax.dynamic_index_in_dim(routers, section_index, 0, keepdims=False)
        return core_block(current, gain_row, router_rows, w_first, w_second, assign)

    def advance_one(moment, carry):
        return advance(moment, combine(moment, carry))

    carry = advance(0, jnp.zeros(init_state.shape[1:], jnp.bfloat16))
    carry = lax.fori_loop(1, total_steps, advance_one, carry)
    return combine(total_steps, carry)[None]


def solution(mesh):
    return jax.shard_map(
        body,
        mesh=mesh,
        in_specs=(
            P(None, ("dp", "expert"), None),
            P(None, ("dp", "expert"), None),
            P(None, "section", None, ("dp", "expert"), None),
            P("section", None),
            P("section", None, None),
            P("section", "expert", "dp", None),
            P("section", "expert", None, "dp"),
        ),
        out_specs=P("section", ("dp", "expert"), None),
        check_vma=False,
    )
```

```python
import jax
import jax.numpy as jnp
from jax import lax
from jax.sharding import PartitionSpec as P

RECUR = 2
CAP = 12


def shifted(block, axis, distance):
    devices = range(lax.axis_size(axis))
    route = [((i - distance) % len(devices), i) for i in devices]
    return lax.ppermute(block, axis, route)


def normalize(current, gain_row):
    as_float = current.astype(jnp.float32)
    inv_rms = lax.rsqrt(jnp.mean(as_float * as_float, axis=-1, keepdims=True) + 1e-05)
    return (as_float * inv_rms * gain_row).astype(jnp.bfloat16)


def expert_rows(item_rows, w_first, w_second):
    extent = item_rows.shape
    flat_rows = item_rows.reshape(-1, extent[-1])
    hidden = jax.nn.gelu(jnp.dot(flat_rows, w_first, preferred_element_type=jnp.float32)).astype(
        jnp.bfloat16
    )
    result = lax.dot_general(
        hidden, w_second, (((1,), (1,)), ((), ())), preferred_element_type=jnp.float32
    ).astype(jnp.bfloat16)
    return result.reshape(extent)


def onward(block, distance):
    sections = lax.axis_size("section")
    experts = lax.axis_size("expert")
    route = [
        (s * experts + e, ((s + 1) % sections) * experts + (e - distance) % experts)
        for s in range(sections)
        for e in range(experts)
    ]
    return lax.ppermute(block, ("section", "expert"), route)


def front(current, gain_row, router_rows, assign):
    tokens = current.shape[0]
    experts = router_rows.shape[0]
    normed = normalize(current, gain_row)
    logits = jnp.dot(normed, router_rows.T, preferred_element_type=jnp.float32)
    labels = lax.broadcasted_iota(jnp.int32, (tokens, experts), 1)
    onehot = (assign[:, None] == labels).astype(jnp.float32)
    gate_value = jax.nn.sigmoid(jnp.sum(onehot * logits, axis=-1))
    earlier = (
        lax.broadcasted_iota(jnp.int32, (tokens, tokens), 0)
        > lax.broadcasted_iota(jnp.int32, (tokens, tokens), 1)
    ).astype(jnp.float32)
    counts = jnp.dot(earlier, onehot, preferred_element_type=jnp.float32)
    slot_index = jnp.sum(onehot * counts, axis=-1).astype(jnp.int32)
    relative = jnp.mod(assign - lax.axis_index("expert"), experts)
    target = relative * CAP + slot_index
    places = (
        lax.broadcasted_iota(jnp.int32, (experts * CAP, tokens), 0) == target[None, :]
    ).astype(jnp.bfloat16)
    return normed, gate_value, places


def core_block(current, gain_row, router_rows, w_first, w_second, assign):
    experts = router_rows.shape[0]
    normed, _, places = front(current, gain_row, router_rows, assign)
    buffer = (
        jnp.dot(places, normed, preferred_element_type=jnp.float32)
        .astype(jnp.bfloat16)
        .reshape(experts, CAP, -1)
    )
    arrived = jnp.stack([buffer[0]] + [shifted(buffer[j], "expert", j) for j in range(1, experts)])
    processed = expert_rows(arrived, w_first, w_second)
    packed = onward(jnp.concatenate([processed[0], current]), 0)
    return (packed,) + tuple(onward(processed[j], j) for j in range(1, experts))


def body(init_state, inject, routes, norm_gain, router, w_up, w_down):
    sections = lax.axis_size("section")
    section_index = lax.axis_index("section")
    rows = w_up.shape[2]
    pieces = jnp.concatenate([w_up[0, 0], jnp.swapaxes(w_down[0, 0], 0, 1)], axis=0)
    both = lax.all_gather(pieces, "dp", axis=0, tiled=False)
    width = norm_gain.shape[-1]
    small = jnp.concatenate(
        [
            norm_gain.reshape(-1),
            router.reshape(-1).astype(jnp.float32),
            routes.reshape(-1).astype(jnp.float32),
        ]
    )
    every = lax.all_gather(small, "section", axis=0, tiled=False)
    gains = every[:, :width]
    routers = every[:, width : width + router.size].reshape((-1,) + router.shape[1:])
    routers = routers.astype(router.dtype)
    all_routes = every[:, width + router.size :].reshape((-1, routes.shape[0]) + routes.shape[2:])
    all_routes = jnp.swapaxes(all_routes, 0, 1).astype(routes.dtype)
    w_first = both[:, :rows].reshape(-1, both.shape[-1])
    w_second = both[:, rows:].reshape(-1, both.shape[-1])
    tokens = init_state.shape[1]
    active_span = sections * RECUR
    total_steps = active_span + sections - 1
    previous_section = jnp.mod(section_index - 1, sections)

    def live_at(moment, section):
        offset = moment - section
        return (offset >= 0) & (offset < active_span)

    def schedule(moment, section):
        clipped = jnp.clip(moment - section, 0, active_span - 1)
        loop_round = clipped // sections
        micro_idx = jnp.mod(sections - 1 - clipped % sections, sections)
        assign = lax.dynamic_slice(
            all_routes, (loop_round, section, micro_idx, 0, 0), (1, 1, 1, tokens, 1)
        ).reshape(tokens)
        return loop_round, micro_idx, assign

    def combine(moment, carry):
        packed, *rest = carry
        slots = packed.shape[0] - tokens
        kept = packed[slots:]
        _, _, assign = schedule(moment - 1, previous_section)
        _, gate_value, places = front(
            kept,
            lax.dynamic_index_in_dim(gains, previous_section, 0, keepdims=False),
            lax.dynamic_index_in_dim(routers, previous_section, 0, keepdims=False),
            assign,
        )
        flat_back = jnp.concatenate([packed[:slots]] + list(rest))
        expert_out = jnp.einsum("st,sd->td", places, flat_back, preferred_element_type=jnp.float32)
        updated = (kept.astype(jnp.float32) + gate_value[:, None] * expert_out).astype(jnp.bfloat16)
        return jnp.where(live_at(moment - 1, previous_section), updated, kept)

    def advance(moment, hidden_state):
        is_live = live_at(moment, section_index)
        loop_round, micro_idx, assign = schedule(moment, section_index)
        initial = lax.dynamic_index_in_dim(init_state, micro_idx, 0, keepdims=False)
        injected_row = lax.dynamic_index_in_dim(inject, micro_idx, 0, keepdims=False)
        incoming = jnp.where(loop_round == 0, initial, hidden_state)
        injected = (incoming.astype(jnp.float32) + injected_row.astype(jnp.float32)).astype(
            jnp.bfloat16
        )
        entering = is_live & (section_index == 0)
        current = jnp.where(entering, injected, hidden_state)
        gain_row = lax.dynamic_index_in_dim(gains, section_index, 0, keepdims=False)
        router_rows = lax.dynamic_index_in_dim(routers, section_index, 0, keepdims=False)
        return core_block(current, gain_row, router_rows, w_first, w_second, assign)

    def advance_one(moment, carry):
        return advance(moment, combine(moment, carry))

    carry = advance(0, jnp.zeros(init_state.shape[1:], jnp.bfloat16))
    carry = lax.fori_loop(1, total_steps, advance_one, carry)
    return combine(total_steps, carry)[None]


def solution(mesh):
    return jax.shard_map(
        body,
        mesh=mesh,
        in_specs=(
            P(None, ("dp", "expert"), None),
            P(None, ("dp", "expert"), None),
            P(None, "section", None, ("dp", "expert"), None),
            P("section", None),
            P("section", None, None),
            P("section", "expert", "dp", None),
            P("section", "expert", None, "dp"),
        ),
        out_specs=P("section", ("dp", "expert"), None),
        check_vma=False,
    )
```

```python
import jax
import jax.numpy as jnp
from jax import lax
from jax.sharding import PartitionSpec as P

RECUR = 2
CAP = 12


def shifted(block, axis, distance):
    devices = range(lax.axis_size(axis))
    route = [((i - distance) % len(devices), i) for i in devices]
    return lax.ppermute(block, axis, route)


def normalize(current, gain_row):
    as_float = current.astype(jnp.float32)
    inv_rms = lax.rsqrt(jnp.mean(as_float * as_float, axis=-1, keepdims=True) + 1e-05)
    return (as_float * inv_rms * gain_row).astype(jnp.bfloat16)


def expert_rows(item_rows, w_first, w_second):
    extent = item_rows.shape
    split_rows = item_rows.reshape((-1,) + w_first.shape[:2])
    hidden = jax.nn.gelu(
        lax.dot_general(
            split_rows, w_first, (((1, 2), (0, 1)), ((), ())), preferred_element_type=jnp.float32
        )
    ).astype(jnp.bfloat16)
    result = lax.dot_general(
        hidden, w_second, (((1,), (2,)), ((), ())), preferred_element_type=jnp.float32
    ).astype(jnp.bfloat16)
    return result.reshape(extent)


def onward(block, distance):
    sections = lax.axis_size("section")
    experts = lax.axis_size("expert")
    route = [
        (s * experts + e, ((s + 1) % sections) * experts + (e - distance) % experts)
        for s in range(sections)
        for e in range(experts)
    ]
    return lax.ppermute(block, ("section", "expert"), route)


def front(current, gain_row, router_rows, assign):
    tokens = current.shape[0]
    experts = router_rows.shape[0]
    normed = normalize(current, gain_row)
    logits = jnp.dot(normed, router_rows.T, preferred_element_type=jnp.float32)
    labels = lax.broadcasted_iota(jnp.int32, (tokens, experts), 1)
    onehot = (assign[:, None] == labels).astype(jnp.float32)
    gate_value = jax.nn.sigmoid(jnp.sum(onehot * logits, axis=-1))
    earlier = (
        lax.broadcasted_iota(jnp.int32, (tokens, tokens), 0)
        > lax.broadcasted_iota(jnp.int32, (tokens, tokens), 1)
    ).astype(jnp.float32)
    counts = jnp.dot(earlier, onehot, preferred_element_type=jnp.float32)
    slot_index = jnp.sum(onehot * counts, axis=-1).astype(jnp.int32)
    relative = jnp.mod(assign - lax.axis_index("expert"), experts)
    target = relative * CAP + slot_index
    places = (
        lax.broadcasted_iota(jnp.int32, (experts * CAP, tokens), 0) == target[None, :]
    ).astype(jnp.bfloat16)
    return normed, gate_value, places


def core_block(current, gain_row, router_rows, w_first, w_second, assign):
    experts = router_rows.shape[0]
    normed, _, places = front(current, gain_row, router_rows, assign)
    buffer = (
        jnp.dot(places, normed, preferred_element_type=jnp.float32)
        .astype(jnp.bfloat16)
        .reshape(experts, CAP, -1)
    )
    arrived = jnp.stack([buffer[0]] + [shifted(buffer[j], "expert", j) for j in range(1, experts)])
    processed = expert_rows(arrived, w_first, w_second)
    packed = onward(jnp.concatenate([processed[0], current]), 0)
    return (packed,) + tuple(onward(processed[j], j) for j in range(1, experts))


def body(init_state, inject, routes, norm_gain, router, w_up, w_down):
    sections = lax.axis_size("section")
    section_index = lax.axis_index("section")
    rows = w_up.shape[2]
    pieces = jnp.concatenate([w_up[0, 0], jnp.swapaxes(w_down[0, 0], 0, 1)], axis=0)
    both = lax.all_gather(pieces, "dp", axis=0, tiled=False)
    gains = lax.all_gather(norm_gain, "section", axis=0, tiled=True)
    routers = lax.all_gather(router, "section", axis=0, tiled=True)
    all_routes = lax.all_gather(routes, "section", axis=1, tiled=True)
    w_first = both[:, :rows]
    w_second = both[:, rows:]
    tokens = init_state.shape[1]
    active_span = sections * RECUR
    total_steps = active_span + sections - 1
    previous_section = jnp.mod(section_index - 1, sections)

    def live_at(moment, section):
        offset = moment - section
        return (offset >= 0) & (offset < active_span)

    def schedule(moment, section):
        clipped = jnp.clip(moment - section, 0, active_span - 1)
        loop_round = clipped // sections
        micro_idx = jnp.mod(sections - 1 - clipped % sections, sections)
        assign = lax.dynamic_slice(
            all_routes, (loop_round, section, micro_idx, 0, 0), (1, 1, 1, tokens, 1)
        ).reshape(tokens)
        return loop_round, micro_idx, assign

    def combine(moment, carry):
        packed, *rest = carry
        slots = packed.shape[0] - tokens
        kept = packed[slots:]
        _, _, assign = schedule(moment - 1, previous_section)
        _, gate_value, places = front(
            kept,
            lax.dynamic_index_in_dim(gains, previous_section, 0, keepdims=False),
            lax.dynamic_index_in_dim(routers, previous_section, 0, keepdims=False),
            assign,
        )
        flat_back = jnp.concatenate([packed[:slots]] + list(rest))
        expert_out = jnp.einsum("st,sd->td", places, flat_back, preferred_element_type=jnp.float32)
        updated = (kept.astype(jnp.float32) + gate_value[:, None] * expert_out).astype(jnp.bfloat16)
        return jnp.where(live_at(moment - 1, previous_section), updated, kept)

    def advance(moment, hidden_state):
        is_live = live_at(moment, section_index)
        loop_round, micro_idx, assign = schedule(moment, section_index)
        initial = lax.dynamic_index_in_dim(init_state, micro_idx, 0, keepdims=False)
        injected_row = lax.dynamic_index_in_dim(inject, micro_idx, 0, keepdims=False)
        incoming = jnp.where(loop_round == 0, initial, hidden_state)
        injected = (incoming.astype(jnp.float32) + injected_row.astype(jnp.float32)).astype(
            jnp.bfloat16
        )
        entering = is_live & (section_index == 0)
        current = jnp.where(entering, injected, hidden_state)
        gain_row = lax.dynamic_index_in_dim(gains, section_index, 0, keepdims=False)
        router_rows = lax.dynamic_index_in_dim(routers, section_index, 0, keepdims=False)
        return core_block(current, gain_row, router_rows, w_first, w_second, assign)

    def advance_one(moment, carry):
        return advance(moment, combine(moment, carry))

    carry = advance(0, jnp.zeros(init_state.shape[1:], jnp.bfloat16))
    carry = lax.fori_loop(1, total_steps, advance_one, carry)
    return combine(total_steps, carry)[None]


def solution(mesh):
    return jax.shard_map(
        body,
        mesh=mesh,
        in_specs=(
            P(None, ("dp", "expert"), None),
            P(None, ("dp", "expert"), None),
            P(None, "section", None, ("dp", "expert"), None),
            P("section", None),
            P("section", None, None),
            P("section", "expert", "dp", None),
            P("section", "expert", None, "dp"),
        ),
        out_specs=P("section", ("dp", "expert"), None),
        check_vma=False,
    )
```
